32 devices in a mesh: phi: 2 (over y), row: 4 (over z), gz: 4 (over x, core).
Axes of the slice: x: 2, y: 2, z: 4, core: 2. Of those that a mesh axis runs over, the one named last changes fastest.
Arguments:
- density: float32 [16, 64, 512], P('phi', 'row', 'gz'), may hold values from -6 to 6
- drift_speed: float32 [3, 64, 512], P(None, 'row', 'gz'), may hold values from -0.5 to 0.5
- viscosity: float32 [64, 512], P('row', 'gz'), may hold values from 0.02 to 0.12
- offsets: int32 [64], P('row'), may hold values from 0 to 15, as said below
Outputs:
- evolved: float32 [16, 64, 512], P('phi', 'row', 'gz')
The draws below stay inside these ranges and needn't reach their ends.
Inputs may be any that keep to these rules, and one draw needn't show every extreme that they name: `offsets`: both 0 and 15 occur.
All inputs are finite; a program needn't handle non-finite values.
Results may differ from the reference program's by a relative error of at most 0.00002.
Values sent between devices are 32-bit elements; how exact they have to be, the bound alone decides.
A program may use at most 64 MiB of HBM per device.

```python
import math
import jax
import jax.numpy as jnp

STEPS = 2
NPHI = 16
NR = 64
NZ = 512


def draw_offsets(key, part):
    shifts_drawn = jax.random.randint(jax.random.fold_in(key, 11), (NR,), 0, NPHI, dtype=jnp.int32)
    picked_rows = jax.random.permutation(jax.random.fold_in(key, 12), NR)
    shifts_drawn = shifts_drawn.at[picked_rows[0]].set(NPHI - 1)
    return shifts_drawn.at[picked_rows[1]].set(0)


def block_scale(own_key, dims, pieces, low, high):
    factor_of, own = 1.0, jax.random.fold_in(own_key, 6)
    for axis_at, shards_of in pieces:
        heights = jnp.exp(jax.random.uniform(jax.random.fold_in(own, axis_at), (shards_of,), jnp.float32, low / len(pieces), high / len(pieces)))
        factor_of = factor_of * jnp.repeat(heights, dims[axis_at] // shards_of).reshape([-1 if axis == axis_at else 1 for axis in range(len(dims))])
    return factor_of


def centred(own_key, dims, spread, limit, pieces=(), kind=jnp.bfloat16):
    result = spread * jax.random.normal(own_key, dims, jnp.float32)
    if pieces:
        result = result * block_scale(own_key, dims, pieces, -0.22, 0.18)
    return jnp.clip(result, -limit, limit).astype(kind)


def setup_inputs(seed: int = 0) -> dict:
    splits = jax.random.split(jax.random.key(seed), 5)
    density = centred(splits[0], (NPHI, NR, NZ), 1.0, 6.0, ((0, 2), (1, 4), (2, 4)), jnp.float32)
    drift_speed = jnp.clip(jax.random.uniform(splits[1], (3, NR, NZ), jnp.float32, -0.5, 0.5) * block_scale(splits[1], (3, NR, NZ), ((1, 4), (2, 4)), -0.4, 0.0), -0.5, 0.5)
    viscosity = jnp.clip(jnp.exp(math.log(0.12) - 1.7917595 * jax.random.uniform(splits[2], (NR, NZ), jnp.float32) ** block_scale(splits[2], (NR, NZ), ((0, 4), (1, 4)), -0.2, 0.2)), 0.02, 0.12)
    offsets = draw_offsets(jax.random.fold_in(splits[4], 71), 0)
    return {"density": density, "drift_speed": drift_speed, "viscosity": viscosity, "offsets": offsets}


def wrapped_pad(values):
    beside_all = jnp.concatenate([values[-2:], values, values[:2]], axis=0)
    return jnp.pad(beside_all, ((0, 0), (2, 2), (2, 2)))


def difference(ahead_one, behind_one, ahead_two, behind_two):
    return (8.0 * (ahead_one - behind_one) - (ahead_two - behind_two)) / 12.0


def tendency(padded, drift_speed, viscosity):
    centre = padded[2:-2, 2:-2, 2:-2]
    phi_ahead = padded[3:-1, 2:-2, 2:-2]
    phi_behind = padded[1:-3, 2:-2, 2:-2]
    rad_ahead = padded[2:-2, 3:-1, 2:-2]
    rad_behind = padded[2:-2, 1:-3, 2:-2]
    hgt_ahead = padded[2:-2, 2:-2, 3:-1]
    hgt_behind = padded[2:-2, 2:-2, 1:-3]
    phi_slope = difference(phi_ahead, phi_behind, padded[4:, 2:-2, 2:-2], padded[:-4, 2:-2, 2:-2])
    rad_slope = difference(rad_ahead, rad_behind, padded[2:-2, 4:, 2:-2], padded[2:-2, :-4, 2:-2])
    hgt_slope = difference(hgt_ahead, hgt_behind, padded[2:-2, 2:-2, 4:], padded[2:-2, 2:-2, :-4])
    neighbours = phi_ahead + phi_behind + rad_ahead + rad_behind + hgt_ahead + hgt_behind
    transport = drift_speed[0] * phi_slope + drift_speed[1] * rad_slope + drift_speed[2] * hgt_slope
    return -transport + viscosity * (neighbours - 6.0 * centre)


def runge_kutta(state, drift_speed, viscosity):
    section_one = state + tendency(wrapped_pad(state), drift_speed, viscosity)
    section_two = 0.75 * state + 0.25 * (section_one + tendency(wrapped_pad(section_one), drift_speed, viscosity))
    return state / 3.0 + (2.0 / 3.0) * (section_two + tendency(wrapped_pad(section_two), drift_speed, viscosity))


def rotate_cycles(state, offsets):
    cell_index = jnp.arange(NPHI, dtype=jnp.int32)
    source = (cell_index[:, None] - offsets[None, :]) % NPHI
    return jnp.take_along_axis(state, jnp.broadcast_to(source[:, :, None], state.shape), axis=0)


def reference(density, drift_speed, viscosity, offsets):
    state = density
    for step_index in range(STEPS):
        state = rotate_cycles(runge_kutta(state, drift_speed, viscosity), offsets)
    return state
```

```python
import functools

import jax
import jax.numpy as jnp
from jax import lax
from jax.experimental import pallas as pl
from jax.experimental.pallas import tpu as pltpu
from jax.sharding import PartitionSpec as P

STEPS = 2
LANES = 128
RIM = 16
MESH = pl.DeviceIdType.MESH


def kernel(
    sizes, dens, drift, visc, offs, out,
    tx, rx, rh, cx, rc, ch, rch, ext, one, two, coef, txo, rxo,
    s_main, r_main, s_rim, r_rim, s_coef, r_coef, s_crim, r_crim, s_out, r_out,
):
    n, nrow, ngz = sizes
    pl_local, rows, _ = dens.shape
    width = LANES // n
    tiles = pl_local // n
    planes = tiles + 2
    nphi = n * pl_local
    p, i, j = lax.axis_index("phi"), lax.axis_index("row"), lax.axis_index("gz")
    count = tiles + 1 if n == 2 else planes

    def row_ok(d):
        return (i + d >= 0) & (i + d < nrow)

    def dev(t, d, g):
        row = i if d == 0 else lax.rem(i + d + nrow, nrow)
        col = j if g == 0 else lax.rem(j + g + ngz, ngz)
        return (t, row, col)

    first, last = p == 0, p == n - 1
    has_up, has_down = j + 1 < ngz, j >= 1

    barrier = pltpu.get_barrier_semaphore()

    def greet(ok, target):
        @pl.when(ok)
        def _():
            pl.semaphore_signal(barrier, inc=1, device_id=target, device_id_type=MESH)

    for k in range(n):
        t = lax.rem(p + k, n)
        for d in (-1, 0, 1):
            if k or d:
                greet(row_ok(d), dev(t, d, 0))
            greet(row_ok(d) & first & has_down, dev(t, d, -1))
            greet(row_ok(d) & last & has_up, dev(t, d, 1))

    lane = lax.broadcasted_iota(jnp.int32, (rows, LANES), 1)
    sub = lax.broadcasted_iota(jnp.int32, (rows, LANES), 0)

    def roll(x, by):
        if isinstance(by, int):
            by = by % LANES
            return x if by == 0 else pltpu.roll(x, by, 1)
        return pltpu.roll(x, lax.rem(by + 4 * LANES, LANES), 1)

    for c in range(3):
        cx[c] = drift[c] * (-1.0 / 12.0)
    cx[3] = visc[...]
    plane = jnp.zeros((rows, LANES), jnp.float32)
    for r in range(rows):
        plane = jnp.where(sub == r, offs[r].astype(jnp.float32), plane)
    cx[4] = plane
    low, high = jnp.zeros((rows, LANES), jnp.float32), jnp.zeros((rows, LANES), jnp.float32)
    for c in range(5):
        here = lane // RIM == c
        low = jnp.where(here, roll(cx[c], c * RIM - (LANES - RIM)), low)
        high = jnp.where(here, roll(cx[c], c * RIM), high)
    ch[0] = low
    ch[1] = high

    for t in range(n):
        for m in range(tiles):
            acc = None
            for s in range(n):
                part = roll(dens[m * n + s], s * width - t * width)
                acc = part if acc is None else jnp.where(lane >= s * width, part, acc)
            tx[t, 1 + m] = acc
        low = high = None
        for q in range(pl_local):
            part_l = roll(dens[q], q * RIM - t * width + RIM)
            part_h = roll(dens[q], q * RIM - t * width - width)
            low = part_l if low is None else jnp.where(lane >= q * RIM, part_l, low)
            high = part_h if high is None else jnp.where(lane >= q * RIM, part_h, high)
        near, far = (high, low) if t == 0 else (low, high)
        tx[t, 0] = near
        tx[t, planes - 1] = far

    expected = jnp.int32(0)
    for d in (-1, 0, 1):
        here = row_ok(d).astype(jnp.int32)
        expected += here * (n - (d == 0))
        expected += here * (j + 1 < ngz).astype(jnp.int32)
        expected += here * (j >= 1).astype(jnp.int32)
    pl.semaphore_wait(barrier, expected)

    def main_copy(k, d):
        t = lax.rem(p + k, n)
        return pltpu.make_async_remote_copy(
            src_ref=tx.at[t, pl.ds(0, count)],
            dst_ref=rx.at[p, 1 - d, pl.ds(0, count)],
            send_sem=s_main.at[k, d + 1], recv_sem=r_main.at[p, 1 - d],
            device_id=dev(t, d, 0), device_id_type=MESH,
        )

    def rim_copy(side, d):
        t, g, at = (0, 1, planes - 1) if side == 0 else (n - 1, -1, planes - 1)
        return pltpu.make_async_remote_copy(
            src_ref=tx.at[t, at], dst_ref=rh.at[p, 1 - d],
            send_sem=s_rim.at[side, d + 1], recv_sem=r_rim.at[p, 1 - d],
            device_id=dev(t, d, g), device_id_type=MESH,
        )

    def coef_copy(d):
        return pltpu.make_async_remote_copy(
            src_ref=cx, dst_ref=rc.at[1 - d],
            send_sem=s_coef.at[d + 1], recv_sem=r_coef.at[1 - d],
            device_id=dev(p, d, 0), device_id_type=MESH,
        )

    def crim_copy(side, d):
        g = 1 if side == 0 else -1
        return pltpu.make_async_remote_copy(
            src_ref=ch.at[side], dst_ref=rch.at[1 - d],
            send_sem=s_crim.at[d + 1], recv_sem=r_crim.at[1 - d],
            device_id=dev(p, d, g), device_id_type=MESH,
        )

    sends = []
    for k in list(range(1, n)) + [0]:
        for d in (-1, 1, 0):
            if k or d:
                sends.append((row_ok(d), functools.partial(main_copy, k, d)))
    for d in (-1, 1):
        sends.append((row_ok(d), functools.partial(coef_copy, d)))
    for d in (-1, 1, 0):
        sends.append((row_ok(d) & has_up, functools.partial(rim_copy, 0, d)))
        sends.append((row_ok(d) & has_down, functools.partial(rim_copy, 1, d)))
        sends.append((row_ok(d) & has_up & first, functools.partial(crim_copy, 0, d)))
        sends.append((row_ok(d) & has_down & last, functools.partial(crim_copy, 1, d)))
    for ok, make in sends:
        @pl.when(ok)
        def _():
            make().start()

    def await_copy(ok, dst, sem):
        @pl.when(ok)
        def _():
            pltpu.make_async_copy(dst, dst, sem).wait()

    out_ok = (first & has_down) | (last & has_up)
    row_at = i * rows + sub
    hgt_at = j * LANES + p * width + lane - RIM
    hgt_in = (hgt_at >= 0) & (hgt_at < ngz * LANES)

    def inside(slot):
        at = row_at + (slot - 1) * rows
        return hgt_in & (at >= 0) & (at < nrow * rows)

    low_side, high_side = lane < RIM, lane >= RIM + width
    swap = (low_side & first) | (high_side & last)

    for slot in (1, 0, 2):
        ok = row_ok(slot - 1)
        if slot != 1:
            await_copy(ok, rc.at[slot], r_coef.at[slot])
        await_copy(ok & out_ok, rch.at[slot], r_crim.at[slot])
        base = jnp.where(first, 0, RIM + width)
        for c in range(5):
            body = cx[c] if slot == 1 else rc[slot, c]
            value = jnp.where(
                swap, roll(rch[slot], base - c * RIM), roll(body, RIM - p * width)
            )
            coef[c, pl.ds(slot * rows, rows)] = jnp.where(inside(slot), value, 0.0)

    for slot in (1, 0, 2):
        ok = row_ok(slot - 1)
        for k in range(n):
            ps = lax.rem(p + k, n)
            mine = k == 0 and slot == 1
            if not mine:
                view = rx.at[ps, slot, pl.ds(0, count)]
                await_copy(ok, view, r_main.at[ps, slot])
            await_copy(ok & out_ok, rh.at[ps, slot], r_rim.at[ps, slot])

            def got(m):
                return tx[p, m] if mine else rx[ps, slot, m]

            rim = rh[ps, slot]
            low = jnp.where(first, rim, got(0))
            high = jnp.where(first, got(0), rim)
            if n > 2:
                high = jnp.where(first | last, high, got(planes - 1))
            for q in range(pl_local):
                m, s = q // n, q % n
                value = jnp.where(
                    low_side, roll(low, -q * RIM),
                    jnp.where(
                        high_side, roll(high, RIM + width - q * RIM),
                        roll(got(1 + m), RIM - s * width),
                    ),
                )
                ext[2 + ps * pl_local + q, pl.ds(slot * rows, rows)] = jnp.where(
                    inside(slot), value, 0.0
                )

    def section(src, dst, r0, size, combine):
        e0, e1, e2, nu = (coef[c, pl.ds(r0, size)] for c in range(4))

        def body(a, carry):
            def at(k, d=0):
                return src[a + 2 + k, pl.ds(r0 + d, size)]

            c = at(0)
            a1, b1, a2, b2 = at(1), at(-1), at(2), at(-2)
            u1, d1, u2, d2 = at(0, 1), at(0, -1), at(0, 2), at(0, -2)
            g1, h1 = pltpu.roll(c, LANES - 1, 1), pltpu.roll(c, 1, 1)
            g2, h2 = pltpu.roll(c, LANES - 2, 1), pltpu.roll(c, 2, 1)
            change = e0 * (8.0 * (a1 - b1) - (a2 - b2))
            change += e1 * (8.0 * (u1 - d1) - (u2 - d2))
            change += e2 * (8.0 * (g1 - h1) - (g2 - h2))
            change += nu * (((a1 + b1) + (u1 + d1)) + (g1 + h1) - 6.0 * c)
            dst[a + 2, pl.ds(r0, size)] = combine(a, c + change)
            return carry

        lax.fori_loop(0, nphi, body, 0)

    def wrap(ref, r0, size):
        at = pl.ds(r0, size)
        ref[pl.ds(0, 2), at] = ref[pl.ds(nphi, 2), at]
        ref[pl.ds(nphi + 2, 2), at] = ref[pl.ds(2, 2), at]

    def rotated(r0):
        value = one[pl.ds(2, nphi), pl.ds(r0, 8)]
        turns = coef[4, pl.ds(r0, 8)].astype(jnp.int32)
        span = 1
        while span < nphi:
            moved = jnp.concatenate([value[nphi - span :], value[: nphi - span]], axis=0)
            value = jnp.where(((turns & span) != 0)[None], moved, value)
            span *= 2
        return value

    for step, (ra, rb, rd) in enumerate((((4, 40), (8, 32), (8, 32)), ((12, 24), (12, 24), (16, 16)))):
        wrap(ext, *ra)
        section(ext, one, *ra, lambda a, v: v)
        wrap(one, *ra)
        section(
            one, two, *rb, lambda a, v: 0.75 * ext[a + 2, pl.ds(rb[0], rb[1])] + 0.25 * v
        )
        wrap(two, *rb)
        section(
            two, one, *rd,
            lambda a, v: ext[a + 2, pl.ds(rd[0], rd[1])] * (1.0 / 3.0) + (2.0 / 3.0) * v,
        )
        for r0 in range(rd[0], rd[0] + rd[1], 8):
            ext[pl.ds(2, nphi), pl.ds(r0, 8)] = rotated(r0)

    def out_copy(k):
        t = lax.rem(p + k, n)
        return pltpu.make_async_remote_copy(
            src_ref=txo.at[k], dst_ref=rxo.at[p],
            send_sem=s_out.at[k], recv_sem=r_out.at[p],
            device_id=dev(t, 0, 0), device_id_type=MESH,
        )

    for k in range(1, n):
        t = lax.rem(p + k, n)
        for m in range(tiles):
            acc = None
            for s in range(n):
                part = roll(
                    ext[2 + t * pl_local + m * n + s, pl.ds(rows, rows)], s * width - RIM
                )
                acc = part if acc is None else jnp.where(lane >= s * width, part, acc)
            txo[k, m] = acc
        out_copy(k).start()

    for q in range(pl_local):
        out[q] = roll(ext[2 + p * pl_local + q, pl.ds(rows, rows)], p * width - RIM)
    for k in range(1, n):
        ps = lax.rem(p + k, n)
        await_copy(True, rxo.at[ps], r_out.at[ps])
        here = (lane >= ps * width) & (lane < (ps + 1) * width)
        for q in range(pl_local):
            m, s = q // n, q % n
            out[q] = jnp.where(here, roll(rxo[ps, m], ps * width - s * width), out[q])
    for ok, make in sends:
        @pl.when(ok)
        def _():
            make().wait_send()
    for k in range(1, n):
        out_copy(k).wait_send()


def local(sizes, density, drift_speed, viscosity, offsets):
    n = sizes[0]
    pl_local, rows, lanes = density.shape
    tiles = pl_local // n
    planes = tiles + 2
    nphi = n * pl_local
    f32 = jnp.float32
    block = (rows, lanes)
    deep = (3 * rows, lanes)
    vmem = pl.BlockSpec(memory_space=pltpu.VMEM)
    dma = pltpu.SemaphoreType.DMA
    return pl.pallas_call(
        functools.partial(kernel, sizes),
        out_shape=jax.ShapeDtypeStruct(density.shape, f32),
        in_specs=[vmem, vmem, vmem, pl.BlockSpec(memory_space=pltpu.SMEM)],
        out_specs=vmem,
        scratch_shapes=[
            pltpu.VMEM((n, planes) + block, f32),
            pltpu.VMEM((n, 3, planes) + block, f32),
            pltpu.VMEM((n, 3) + block, f32),
            pltpu.VMEM((5,) + block, f32),
            pltpu.VMEM((3, 5) + block, f32),
            pltpu.VMEM((2,) + block, f32),
            pltpu.VMEM((3,) + block, f32),
            pltpu.VMEM((nphi + 4,) + deep, f32),
            pltpu.VMEM((nphi + 4,) + deep, f32),
            pltpu.VMEM((nphi + 4,) + deep, f32),
            pltpu.VMEM((5,) + deep, f32),
            pltpu.VMEM((n, tiles) + block, f32),
            pltpu.VMEM((n, tiles) + block, f32),
            dma((n, 3)), dma((n, 3)), dma((2, 3)), dma((n, 3)), dma((3,)), dma((3,)),
            dma((3,)), dma((3,)), dma((n,)), dma((n,)),
        ],
        compiler_params=pltpu.CompilerParams(
            collective_id=0, has_side_effects=True, vmem_limit_bytes=32 * 1024 * 1024
        ),
    )(density, drift_speed, viscosity, offsets)


def solution(mesh):
    sizes = (mesh.shape["phi"], mesh.shape["row"], mesh.shape["gz"])
    in_specs = (P("phi", "row", "gz"), P(None, "row", "gz"), P("row", "gz"), P("row"))
    return jax.shard_map(
        functools.partial(local, sizes), mesh=mesh, in_specs=in_specs,
        out_specs=P("phi", "row", "gz"), check_vma=False,
    )
```

```python
import functools

import jax
import jax.numpy as jnp
from jax import lax
from jax.experimental import pallas as pl
from jax.experimental.pallas import tpu as pltpu
from jax.sharding import PartitionSpec as P

STEPS = 2
LANES = 128
RIM = 16
MESH = pl.DeviceIdType.MESH


def kernel(
    sizes, dens_in, drift_in, visc_in, offs_in, out, dens, drift, visc, offs, s_in,
    tx, rx, rh, cx, rc, ch, rch, ext, one, two, coef, txo, rxo,
    s_main, r_main, s_rim, r_rim, s_coef, r_coef, s_crim, r_crim, s_out, r_out,
):
    n, nrow, ngz = sizes
    loads = [
        pltpu.make_async_copy(src, dst, s_in.at[at])
        for at, (src, dst) in enumerate(
            ((offs_in, offs), (drift_in, drift), (visc_in, visc), (dens_in, dens))
        )
    ]
    for load in loads:
        load.start()
    pl_local, rows, _ = dens.shape
    width = LANES // n
    tiles = pl_local // n
    planes = tiles + 2
    nphi = n * pl_local
    p, i, j = lax.axis_index("phi"), lax.axis_index("row"), lax.axis_index("gz")
    count = tiles + 1 if n == 2 else planes

    def row_ok(d):
        return (i + d >= 0) & (i + d < nrow)

    def dev(t, d, g):
        row = i if d == 0 else lax.rem(i + d + nrow, nrow)
        col = j if g == 0 else lax.rem(j + g + ngz, ngz)
        return (t, row, col)

    first, last = p == 0, p == n - 1
    has_up, has_down = j + 1 < ngz, j >= 1

    barrier = pltpu.get_barrier_semaphore()

    def greet(ok, target):
        @pl.when(ok)
        def _():
            pl.semaphore_signal(barrier, inc=1, device_id=target, device_id_type=MESH)

    for k in range(n):
        t = lax.rem(p + k, n)
        for d in (-1, 0, 1):
            if k or d:
                greet(row_ok(d), dev(t, d, 0))
            greet(row_ok(d) & first & has_down, dev(t, d, -1))
            greet(row_ok(d) & last & has_up, dev(t, d, 1))

    lane = lax.broadcasted_iota(jnp.int32, (rows, LANES), 1)
    sub = lax.broadcasted_iota(jnp.int32, (rows, LANES), 0)

    def roll(x, by):
        if isinstance(by, int):
            by = by % LANES
            return x if by == 0 else pltpu.roll(x, by, 1)
        return pltpu.roll(x, lax.rem(by + 4 * LANES, LANES), 1)

    for load in loads[:3]:
        load.wait()
    for c in range(3):
        cx[c] = drift[c] * (-1.0 / 12.0)
    cx[3] = visc[...]
    plane = jnp.zeros((rows, LANES), jnp.float32)
    for r in range(rows):
        plane = jnp.where(sub == r, offs[r].astype(jnp.float32), plane)
    cx[4] = plane
    low, high = jnp.zeros((rows, LANES), jnp.float32), jnp.zeros((rows, LANES), jnp.float32)
    for c in range(5):
        here = lane // RIM == c
        low = jnp.where(here, roll(cx[c], c * RIM - (LANES - RIM)), low)
        high = jnp.where(here, roll(cx[c], c * RIM), high)
    ch[0] = low
    ch[1] = high

    loads[3].wait()
    for t in range(n):
        for m in range(tiles):
            acc = None
            for s in range(n):
                part = roll(dens[m * n + s], s * width - t * width)
                acc = part if acc is None else jnp.where(lane >= s * width, part, acc)
            tx[t, 1 + m] = acc
        low = high = None
        for q in range(pl_local):
            part_l = roll(dens[q], q * RIM - t * width + RIM)
            part_h = roll(dens[q], q * RIM - t * width - width)
            low = part_l if low is None else jnp.where(lane >= q * RIM, part_l, low)
            high = part_h if high is None else jnp.where(lane >= q * RIM, part_h, high)
        near, far = (high, low) if t == 0 else (low, high)
        tx[t, 0] = near
        tx[t, planes - 1] = far

    expected = jnp.int32(0)
    for d in (-1, 0, 1):
        here = row_ok(d).astype(jnp.int32)
        expected += here * (n - (d == 0))
        expected += here * (j + 1 < ngz).astype(jnp.int32)
        expected += here * (j >= 1).astype(jnp.int32)
    pl.semaphore_wait(barrier, expected)

    def main_copy(k, d):
        t = lax.rem(p + k, n)
        return pltpu.make_async_remote_copy(
            src_ref=tx.at[t, pl.ds(0, count)],
            dst_ref=rx.at[p, 1 - d, pl.ds(0, count)],
            send_sem=s_main.at[k, d + 1], recv_sem=r_main.at[p, 1 - d],
            device_id=dev(t, d, 0), device_id_type=MESH,
        )

    def rim_copy(side, d):
        t, g, at = (0, 1, planes - 1) if side == 0 else (n - 1, -1, planes - 1)
        return pltpu.make_async_remote_copy(
            src_ref=tx.at[t, at], dst_ref=rh.at[p, 1 - d],
            send_sem=s_rim.at[side, d + 1], recv_sem=r_rim.at[p, 1 - d],
            device_id=dev(t, d, g), device_id_type=MESH,
        )

    def coef_copy(d):
        return pltpu.make_async_remote_copy(
            src_ref=cx, dst_ref=rc.at[1 - d],
            send_sem=s_coef.at[d + 1], recv_sem=r_coef.at[1 - d],
            device_id=dev(p, d, 0), device_id_type=MESH,
        )

    def crim_copy(side, d):
        g = 1 if side == 0 else -1
        return pltpu.make_async_remote_copy(
            src_ref=ch.at[side], dst_ref=rch.at[1 - d],
            send_sem=s_crim.at[d + 1], recv_sem=r_crim.at[1 - d],
            device_id=dev(p, d, g), device_id_type=MESH,
        )

    sends = []
    for k in list(range(1, n)) + [0]:
        for d in (-1, 1, 0):
            if k or d:
                sends.append((row_ok(d), functools.partial(main_copy, k, d)))
    for d in (-1, 1):
        sends.append((row_ok(d), functools.partial(coef_copy, d)))
    for d in (-1, 1, 0):
        sends.append((row_ok(d) & has_up, functools.partial(rim_copy, 0, d)))
        sends.append((row_ok(d) & has_down, functools.partial(rim_copy, 1, d)))
        sends.append((row_ok(d) & has_up & first, functools.partial(crim_copy, 0, d)))
        sends.append((row_ok(d) & has_down & last, functools.partial(crim_copy, 1, d)))
    for ok, make in sends:
        @pl.when(ok)
        def _():
            make().start()

    def await_copy(ok, dst, sem):
        @pl.when(ok)
        def _():
            pltpu.make_async_copy(dst, dst, sem).wait()

    out_ok = (first & has_down) | (last & has_up)
    row_at = i * rows + sub
    hgt_at = j * LANES + p * width + lane - RIM
    hgt_in = (hgt_at >= 0) & (hgt_at < ngz * LANES)

    def inside(slot):
        at = row_at + (slot - 1) * rows
        return hgt_in & (at >= 0) & (at < nrow * rows)

    low_side, high_side = lane < RIM, lane >= RIM + width
    swap = (low_side & first) | (high_side & last)

    for slot in (1, 0, 2):
        ok = row_ok(slot - 1)
        if slot != 1:
            await_copy(ok, rc.at[slot], r_coef.at[slot])
        await_copy(ok & out_ok, rch.at[slot], r_crim.at[slot])
        base = jnp.where(first, 0, RIM + width)
        for c in range(5):
            body = cx[c] if slot == 1 else rc[slot, c]
            value = jnp.where(
                swap, roll(rch[slot], base - c * RIM), roll(body, RIM - p * width)
            )
            coef[c, pl.ds(slot * rows, rows)] = jnp.where(inside(slot), value, 0.0)

    for slot in (1, 0, 2):
        ok = row_ok(slot - 1)
        for k in range(n):
            ps = lax.rem(p + k, n)
            mine = k == 0 and slot == 1
            if not mine:
                view = rx.at[ps, slot, pl.ds(0, count)]
                await_copy(ok, view, r_main.at[ps, slot])
            await_copy(ok & out_ok, rh.at[ps, slot], r_rim.at[ps, slot])

            def got(m):
                return tx[p, m] if mine else rx[ps, slot, m]

            rim = rh[ps, slot]
            low = jnp.where(first, rim, got(0))
            high = jnp.where(first, got(0), rim)
            if n > 2:
                high = jnp.where(first | last, high, got(planes - 1))
            for q in range(pl_local):
                m, s = q // n, q % n
                value = jnp.where(
                    low_side, roll(low, -q * RIM),
                    jnp.where(
                        high_side, roll(high, RIM + width - q * RIM),
                        roll(got(1 + m), RIM - s * width),
                    ),
                )
                ext[2 + ps * pl_local + q, pl.ds(slot * rows, rows)] = jnp.where(
                    inside(slot), value, 0.0
                )

    def section(src, dst, r0, size, combine):
        e0, e1, e2, nu = (coef[c, pl.ds(r0, size)] for c in range(4))

        def body(a, carry):
            def at(k, d=0):
                return src[a + 2 + k, pl.ds(r0 + d, size)]

            c = at(0)
            a1, b1, a2, b2 = at(1), at(-1), at(2), at(-2)
            u1, d1, u2, d2 = at(0, 1), at(0, -1), at(0, 2), at(0, -2)
            g1, h1 = pltpu.roll(c, LANES - 1, 1), pltpu.roll(c, 1, 1)
            g2, h2 = pltpu.roll(c, LANES - 2, 1), pltpu.roll(c, 2, 1)
            change = e0 * (8.0 * (a1 - b1) - (a2 - b2))
            change += e1 * (8.0 * (u1 - d1) - (u2 - d2))
            change += e2 * (8.0 * (g1 - h1) - (g2 - h2))
            change += nu * (((a1 + b1) + (u1 + d1)) + (g1 + h1) - 6.0 * c)
            dst[a + 2, pl.ds(r0, size)] = combine(a, c + change)
            return carry

        lax.fori_loop(0, nphi, body, 0, unroll=16 if nphi % 16 == 0 else 1)

    def wrap(ref, r0, size):
        at = pl.ds(r0, size)
        ref[pl.ds(0, 2), at] = ref[pl.ds(nphi, 2), at]
        ref[pl.ds(nphi + 2, 2), at] = ref[pl.ds(2, 2), at]

    def rotated(r0):
        value = one[pl.ds(2, nphi), pl.ds(r0, 8)]
        turns = coef[4, pl.ds(r0, 8)].astype(jnp.int32)
        span = 1
        while span < nphi:
            moved = jnp.concatenate([value[nphi - span :], value[: nphi - span]], axis=0)
            value = jnp.where(((turns & span) != 0)[None], moved, value)
            span *= 2
        return value

    for step, (ra, rb, rd) in enumerate((((4, 40), (8, 32), (8, 32)), ((12, 24), (12, 24), (16, 16)))):
        wrap(ext, *ra)
        section(ext, one, *ra, lambda a, v: v)
        wrap(one, *ra)
        section(
            one, two, *rb, lambda a, v: 0.75 * ext[a + 2, pl.ds(rb[0], rb[1])] + 0.25 * v
        )
        wrap(two, *rb)
        section(
            two, one, *rd,
            lambda a, v: ext[a + 2, pl.ds(rd[0], rd[1])] * (1.0 / 3.0) + (2.0 / 3.0) * v,
        )
        for r0 in range(rd[0], rd[0] + rd[1], 8):
            ext[pl.ds(2, nphi), pl.ds(r0, 8)] = rotated(r0)

    def out_copy(k):
        t = lax.rem(p + k, n)
        return pltpu.make_async_remote_copy(
            src_ref=txo.at[k], dst_ref=rxo.at[p],
            send_sem=s_out.at[k], recv_sem=r_out.at[p],
            device_id=dev(t, 0, 0), device_id_type=MESH,
        )

    for k in range(1, n):
        t = lax.rem(p + k, n)
        for m in range(tiles):
            acc = None
            for s in range(n):
                part = roll(
                    ext[2 + t * pl_local + m * n + s, pl.ds(rows, rows)], s * width - RIM
                )
                acc = part if acc is None else jnp.where(lane >= s * width, part, acc)
            txo[k, m] = acc
        out_copy(k).start()

    for q in range(pl_local):
        out[q] = roll(ext[2 + p * pl_local + q, pl.ds(rows, rows)], p * width - RIM)
    for k in range(1, n):
        ps = lax.rem(p + k, n)
        await_copy(True, rxo.at[ps], r_out.at[ps])
        here = (lane >= ps * width) & (lane < (ps + 1) * width)
        for q in range(pl_local):
            m, s = q // n, q % n
            out[q] = jnp.where(here, roll(rxo[ps, m], ps * width - s * width), out[q])
    for ok, make in sends:
        @pl.when(ok)
        def _():
            make().wait_send()
    for k in range(1, n):
        out_copy(k).wait_send()


def local(sizes, density, drift_speed, viscosity, offsets):
    n = sizes[0]
    pl_local, rows, lanes = density.shape
    tiles = pl_local // n
    planes = tiles + 2
    nphi = n * pl_local
    f32 = jnp.float32
    block = (rows, lanes)
    deep = (3 * rows, lanes)
    vmem = pl.BlockSpec(memory_space=pltpu.VMEM)
    dma = pltpu.SemaphoreType.DMA
    return pl.pallas_call(
        functools.partial(kernel, sizes),
        out_shape=jax.ShapeDtypeStruct(density.shape, f32),
        in_specs=[pl.BlockSpec(memory_space=pltpu.HBM)] * 4,
        out_specs=vmem,
        scratch_shapes=[
            pltpu.VMEM(density.shape, f32),
            pltpu.VMEM(drift_speed.shape, f32),
            pltpu.VMEM(viscosity.shape, f32),
            pltpu.SMEM(offsets.shape, jnp.int32),
            dma((4,)),
            pltpu.VMEM((n, planes) + block, f32),
            pltpu.VMEM((n, 3, planes) + block, f32),
            pltpu.VMEM((n, 3) + block, f32),
            pltpu.VMEM((5,) + block, f32),
            pltpu.VMEM((3, 5) + block, f32),
            pltpu.VMEM((2,) + block, f32),
            pltpu.VMEM((3,) + block, f32),
            pltpu.VMEM((nphi + 4,) + deep, f32),
            pltpu.VMEM((nphi + 4,) + deep, f32),
            pltpu.VMEM((nphi + 4,) + deep, f32),
            pltpu.VMEM((5,) + deep, f32),
            pltpu.VMEM((n, tiles) + block, f32),
            pltpu.VMEM((n, tiles) + block, f32),
            dma((n, 3)), dma((n, 3)), dma((2, 3)), dma((n, 3)), dma((3,)), dma((3,)),
            dma((3,)), dma((3,)), dma((n,)), dma((n,)),
        ],
        compiler_params=pltpu.CompilerParams(
            collective_id=0, has_side_effects=True, vmem_limit_bytes=32 * 1024 * 1024
        ),
    )(density, drift_speed, viscosity, offsets)


def solution(mesh):
    sizes = (mesh.shape["phi"], mesh.shape["row"], mesh.shape["gz"])
    in_specs = (P("phi", "row", "gz"), P(None, "row", "gz"), P("row", "gz"), P("row"))
    return jax.shard_map(
        functools.partial(local, sizes), mesh=mesh, in_specs=in_specs,
        out_specs=P("phi", "row", "gz"), check_vma=False,
    )
```

```python
import functools

import jax
import jax.numpy as jnp
from jax import lax
from jax.experimental import pallas as pl
from jax.experimental.pallas import tpu as pltpu
from jax.sharding import PartitionSpec as P

STEPS = 2
LANES = 128
RIM = 16
MESH = pl.DeviceIdType.MESH


def kernel(
    sizes, dens_in, drift_in, visc_in, offs_in, out, dens, drift, visc, offs, s_in,
    tx, rx, rh, cx, rc, ch, rch, ext, one, two, coef, txo, rxo,
    s_main, r_main, s_rim, r_rim, s_coef, r_coef, s_crim, r_crim, s_out, r_out,
):
    n, nrow, ngz = sizes
    loads = [
        pltpu.make_async_copy(src, dst, s_in.at[at])
        for at, (src, dst) in enumerate(
            ((offs_in, offs), (drift_in, drift), (visc_in, visc), (dens_in, dens))
        )
    ]
    for load in loads:
        load.start()
    pl_local, rows, _ = dens.shape
    width = LANES // n
    tiles = pl_local // n
    planes = tiles + 2
    nphi = n * pl_local
    p, i, j = lax.axis_index("phi"), lax.axis_index("row"), lax.axis_index("gz")
    count = tiles + 1 if n == 2 else planes

    def row_ok(d):
        return (i + d >= 0) & (i + d < nrow)

    def dev(t, d, g):
        row = i if d == 0 else lax.rem(i + d + nrow, nrow)
        col = j if g == 0 else lax.rem(j + g + ngz, ngz)
        return (t, row, col)

    first, last = p == 0, p == n - 1
    has_up, has_down = j + 1 < ngz, j >= 1

    barrier = pltpu.get_barrier_semaphore()

    def greet(ok, target):
        @pl.when(ok)
        def _():
            pl.semaphore_signal(barrier, inc=1, device_id=target, device_id_type=MESH)

    for k in range(n):
        t = lax.rem(p + k, n)
        for d in (-1, 0, 1):
            if k or d:
                greet(row_ok(d), dev(t, d, 0))
            greet(row_ok(d) & first & has_down, dev(t, d, -1))
            greet(row_ok(d) & last & has_up, dev(t, d, 1))

    lane = lax.broadcasted_iota(jnp.int32, (rows, LANES), 1)
    sub = lax.broadcasted_iota(jnp.int32, (rows, LANES), 0)

    def roll(x, by):
        if isinstance(by, int):
            by = by % LANES
            return x if by == 0 else pltpu.roll(x, by, 1)
        return pltpu.roll(x, lax.rem(by + 4 * LANES, LANES), 1)

    for load in loads[:3]:
        load.wait()
    for c in range(3):
        cx[c] = drift[c] * (-1.0 / 12.0)
    cx[3] = visc[...]
    plane = jnp.zeros((rows, LANES), jnp.float32)
    for r in range(rows):
        plane = jnp.where(sub == r, offs[r].astype(jnp.float32), plane)
    cx[4] = plane
    low, high = jnp.zeros((rows, LANES), jnp.float32), jnp.zeros((rows, LANES), jnp.float32)
    for c in range(5):
        here = lane // RIM == c
        low = jnp.where(here, roll(cx[c], c * RIM - (LANES - RIM)), low)
        high = jnp.where(here, roll(cx[c], c * RIM), high)
    ch[0] = low
    ch[1] = high

    loads[3].wait()
    for t in range(n):
        for m in range(tiles):
            acc = None
            for s in range(n):
                part = roll(dens[m * n + s], s * width - t * width)
                acc = part if acc is None else jnp.where(lane >= s * width, part, acc)
            tx[t, 1 + m] = acc
        low = high = None
        for q in range(pl_local):
            part_l = roll(dens[q], q * RIM - t * width + RIM)
            part_h = roll(dens[q], q * RIM - t * width - width)
            low = part_l if low is None else jnp.where(lane >= q * RIM, part_l, low)
            high = part_h if high is None else jnp.where(lane >= q * RIM, part_h, high)
        near, far = (high, low) if t == 0 else (low, high)
        tx[t, 0] = near
        tx[t, planes - 1] = far

    expected = jnp.int32(0)
    for d in (-1, 0, 1):
        here = row_ok(d).astype(jnp.int32)
        expected += here * (n - (d == 0))
        expected += here * (j + 1 < ngz).astype(jnp.int32)
        expected += here * (j >= 1).astype(jnp.int32)
    pl.semaphore_wait(barrier, expected)

    def main_copy(k, d):
        t = lax.rem(p + k, n)
        return pltpu.make_async_remote_copy(
            src_ref=tx.at[t, pl.ds(0, count)],
            dst_ref=rx.at[p, 1 - d, pl.ds(0, count)],
            send_sem=s_main.at[k, d + 1], recv_sem=r_main.at[p, 1 - d],
            device_id=dev(t, d, 0), device_id_type=MESH,
        )

    def rim_copy(side, d):
        t, g, at = (0, 1, planes - 1) if side == 0 else (n - 1, -1, planes - 1)
        return pltpu.make_async_remote_copy(
            src_ref=tx.at[t, at], dst_ref=rh.at[p, 1 - d],
            send_sem=s_rim.at[side, d + 1], recv_sem=r_rim.at[p, 1 - d],
            device_id=dev(t, d, g), device_id_type=MESH,
        )

    def coef_copy(d):
        return pltpu.make_async_remote_copy(
            src_ref=cx, dst_ref=rc.at[1 - d],
            send_sem=s_coef.at[d + 1], recv_sem=r_coef.at[1 - d],
            device_id=dev(p, d, 0), device_id_type=MESH,
        )

    def crim_copy(side, d):
        g = 1 if side == 0 else -1
        return pltpu.make_async_remote_copy(
            src_ref=ch.at[side], dst_ref=rch.at[1 - d],
            send_sem=s_crim.at[d + 1], recv_sem=r_crim.at[1 - d],
            device_id=dev(p, d, g), device_id_type=MESH,
        )

    sends = []
    for k in list(range(1, n)) + [0]:
        for d in (-1, 1, 0):
            if k or d:
                sends.append((row_ok(d), functools.partial(main_copy, k, d)))
    for d in (-1, 1):
        sends.append((row_ok(d), functools.partial(coef_copy, d)))
    for d in (-1, 1, 0):
        sends.append((row_ok(d) & has_up, functools.partial(rim_copy, 0, d)))
        sends.append((row_ok(d) & has_down, functools.partial(rim_copy, 1, d)))
        sends.append((row_ok(d) & has_up & first, functools.partial(crim_copy, 0, d)))
        sends.append((row_ok(d) & has_down & last, functools.partial(crim_copy, 1, d)))
    for ok, make in sends:
        @pl.when(ok)
        def _():
            make().start()

    def await_copy(ok, dst, sem):
        @pl.when(ok)
        def _():
            pltpu.make_async_copy(dst, dst, sem).wait()

    out_ok = (first & has_down) | (last & has_up)
    row_at = i * rows + sub
    hgt_at = j * LANES + p * width + lane - RIM
    hgt_in = (hgt_at >= 0) & (hgt_at < ngz * LANES)

    def inside(slot):
        at = row_at + (slot - 1) * rows
        return hgt_in & (at >= 0) & (at < nrow * rows)

    low_side, high_side = lane < RIM, lane >= RIM + width
    swap = (low_side & first) | (high_side & last)

    for slot in (1, 0, 2):
        ok = row_ok(slot - 1)
        if slot != 1:
            await_copy(ok, rc.at[slot], r_coef.at[slot])
        await_copy(ok & out_ok, rch.at[slot], r_crim.at[slot])
        base = jnp.where(first, 0, RIM + width)
        for c in range(5):
            body = cx[c] if slot == 1 else rc[slot, c]
            value = jnp.where(
                swap, roll(rch[slot], base - c * RIM), roll(body, RIM - p * width)
            )
            coef[c, pl.ds(slot * rows, rows)] = jnp.where(inside(slot), value, 0.0)

    for slot in (1, 0, 2):
        ok = row_ok(slot - 1)
        for k in range(n):
            ps = lax.rem(p + k, n)
            mine = k == 0 and slot == 1
            if not mine:
                view = rx.at[ps, slot, pl.ds(0, count)]
                await_copy(ok, view, r_main.at[ps, slot])
            await_copy(ok & out_ok, rh.at[ps, slot], r_rim.at[ps, slot])

            def got(m):
                return tx[p, m] if mine else rx[ps, slot, m]

            rim = rh[ps, slot]
            low = jnp.where(first, rim, got(0))
            high = jnp.where(first, got(0), rim)
            if n > 2:
                high = jnp.where(first | last, high, got(planes - 1))
            for q in range(pl_local):
                m, s = q // n, q % n
                value = jnp.where(
                    low_side, roll(low, -q * RIM),
                    jnp.where(
                        high_side, roll(high, RIM + width - q * RIM),
                        roll(got(1 + m), RIM - s * width),
                    ),
                )
                ext[2 + ps * pl_local + q, pl.ds(slot * rows, rows)] = jnp.where(
                    inside(slot), value, 0.0
                )

    def section(src, dst, r0, size, combine):
        e0, e1, e2, nu = (coef[c, pl.ds(r0, size)] for c in range(4))

        def body(a, carry):
            def at(k, d=0):
                return src[a + 2 + k, pl.ds(r0 + d, size)]

            c = at(0)
            a1, b1, a2, b2 = at(1), at(-1), at(2), at(-2)
            u1, d1, u2, d2 = at(0, 1), at(0, -1), at(0, 2), at(0, -2)
            g1, h1 = pltpu.roll(c, LANES - 1, 1), pltpu.roll(c, 1, 1)
            g2, h2 = pltpu.roll(c, LANES - 2, 1), pltpu.roll(c, 2, 1)
            change = e0 * (8.0 * (a1 - b1) - (a2 - b2))
            change += e1 * (8.0 * (u1 - d1) - (u2 - d2))
            change += e2 * (8.0 * (g1 - h1) - (g2 - h2))
            change += nu * (((a1 + b1) + (u1 + d1)) + (g1 + h1) - 6.0 * c)
            dst[a + 2, pl.ds(r0, size)] = combine(a, c + change)
            return carry

        lax.fori_loop(0, nphi, body, 0, unroll=16 if nphi % 16 == 0 else 1)

    def wrap(ref, r0, size):
        at = pl.ds(r0, size)
        ref[pl.ds(0, 2), at] = ref[pl.ds(nphi, 2), at]
        ref[pl.ds(nphi + 2, 2), at] = ref[pl.ds(2, 2), at]

    def rotated(r0):
        value = one[pl.ds(2, nphi), pl.ds(r0, 8)]
        turns = coef[4, pl.ds(r0, 8)].astype(jnp.int32)
        span = 1
        while span < nphi:
            moved = jnp.concatenate([value[nphi - span :], value[: nphi - span]], axis=0)
            value = jnp.where(((turns & span) != 0)[None], moved, value)
            span *= 2
        return value

    for step, (ra, rb, rd) in enumerate((((4, 40), (8, 32), (8, 32)), ((12, 24), (12, 24), (16, 16)))):
        wrap(ext, *ra)
        section(ext, one, *ra, lambda a, v: v)
        wrap(one, *ra)
        section(
            one, two, *rb, lambda a, v: 0.75 * ext[a + 2, pl.ds(rb[0], rb[1])] + 0.25 * v
        )
        wrap(two, *rb)
        section(
            two, one, *rd,
            lambda a, v: ext[a + 2, pl.ds(rd[0], rd[1])] * (1.0 / 3.0) + (2.0 / 3.0) * v,
        )
        for r0 in range(rd[0], rd[0] + rd[1], 8):
            ext[pl.ds(2, nphi), pl.ds(r0, 8)] = rotated(r0)

    def out_copy(k):
        t = lax.rem(p + k, n)
        return pltpu.make_async_remote_copy(
            src_ref=txo.at[k], dst_ref=rxo.at[p],
            send_sem=s_out.at[k], recv_sem=r_out.at[p],
            device_id=dev(t, 0, 0), device_id_type=MESH,
        )

    for k in range(1, n):
        t = lax.rem(p + k, n)
        for m in range(tiles):
            acc = None
            for s in range(n):
                part = roll(
                    ext[2 + t * pl_local + m * n + s, pl.ds(rows, rows)], s * width - RIM
                )
                acc = part if acc is None else jnp.where(lane >= s * width, part, acc)
            txo[k, m] = acc
        out_copy(k).start()

    for q in range(pl_local):
        out[q] = roll(ext[2 + p * pl_local + q, pl.ds(rows, rows)], p * width - RIM)
    for k in range(1, n):
        ps = lax.rem(p + k, n)
        await_copy(True, rxo.at[ps], r_out.at[ps])
        here = (lane >= ps * width) & (lane < (ps + 1) * width)
        for q in range(pl_local):
            m, s = q // n, q % n
            out[q] = jnp.where(here, roll(rxo[ps, m], ps * width - s * width), out[q])
    for ok, make in sends:
        @pl.when(ok)
        def _():
            make().wait_send()
    for k in range(1, n):
        out_copy(k).wait_send()


def local(sizes, density, drift_speed, viscosity, offsets):
    n = sizes[0]
    pl_local, rows, lanes = density.shape
    tiles = pl_local // n
    planes = tiles + 2
    nphi = n * pl_local
    f32 = jnp.float32
    block = (rows, lanes)
    deep = (3 * rows, lanes)
    vmem = pl.BlockSpec(memory_space=pltpu.VMEM)
    dma = pltpu.SemaphoreType.DMA
    return pl.pallas_call(
        functools.partial(kernel, sizes),
        out_shape=jax.ShapeDtypeStruct(density.shape, f32),
        in_specs=[pl.BlockSpec(memory_space=pltpu.HBM)] * 4,
        out_specs=vmem,
        scratch_shapes=[
            pltpu.VMEM(density.shape, f32),
            pltpu.VMEM(drift_speed.shape, f32),
            pltpu.VMEM(viscosity.shape, f32),
            pltpu.SMEM(offsets.shape, jnp.int32),
            dma((4,)),
            pltpu.VMEM((n, planes) + block, f32),
            pltpu.VMEM((n, 3, planes) + block, f32),
            pltpu.VMEM((n, 3) + block, f32),
            pltpu.VMEM((5,) + block, f32),
            pltpu.VMEM((3, 5) + block, f32),
            pltpu.VMEM((2,) + block, f32),
            pltpu.VMEM((3,) + block, f32),
            pltpu.VMEM((nphi + 4,) + deep, f32),
            pltpu.VMEM((nphi + 4,) + deep, f32),
            pltpu.VMEM((nphi + 4,) + deep, f32),
            pltpu.VMEM((5,) + deep, f32),
            pltpu.VMEM((n, tiles) + block, f32),
            pltpu.VMEM((n, tiles) + block, f32),
            dma((n, 3)), dma((n, 3)), dma((2, 3)), dma((n, 3)), dma((3,)), dma((3,)),
            dma((3,)), dma((3,)), dma((n,)), dma((n,)),
        ],
        compiler_params=pltpu.CompilerParams(
            collective_id=0, has_side_effects=True, vmem_limit_bytes=60 * 1024 * 1024
        ),
    )(density, drift_speed, viscosity, offsets)


def solution(mesh):
    sizes = (mesh.shape["phi"], mesh.shape["row"], mesh.shape["gz"])
    in_specs = (P("phi", "row", "gz"), P(None, "row", "gz"), P("row", "gz"), P("row"))
    return jax.shard_map(
        functools.partial(local, sizes), mesh=mesh, in_specs=in_specs,
        out_specs=P("phi", "row", "gz"), check_vma=False,
    )
```

```python
import functools

import jax
import jax.numpy as jnp
from jax import lax
from jax.experimental import pallas as pl
from jax.experimental.pallas import tpu as pltpu
from jax.sharding import PartitionSpec as P

STEPS = 2
LANES = 128
RIM = 16
MESH = pl.DeviceIdType.MESH


def kernel(
    sizes, dens_in, drift_in, visc_in, offs_in, out, dens, drift, visc, offs, s_in,
    tx, rx, rh, cx, rc, ch, rch, ext, one, two, coef, txo, rxo,
    s_main, r_main, s_rim, r_rim, s_coef, r_coef, s_crim, r_crim, s_out, r_out,
):
    n, nrow, ngz = sizes
    loads = [
        pltpu.make_async_copy(src, dst, s_in.at[at])
        for at, (src, dst) in enumerate(
            ((offs_in, offs), (drift_in, drift), (visc_in, visc), (dens_in, dens))
        )
    ]
    for load in loads:
        load.start()
    pl_local, rows, _ = dens.shape
    width = LANES // n
    tiles = pl_local // n
    planes = tiles + 2
    nphi = n * pl_local
    p, i, j = lax.axis_index("phi"), lax.axis_index("row"), lax.axis_index("gz")
    count = tiles + 1 if n == 2 else planes

    def row_ok(d):
        return (i + d >= 0) & (i + d < nrow)

    def dev(t, d, g):
        row = i if d == 0 else lax.rem(i + d + nrow, nrow)
        col = j if g == 0 else lax.rem(j + g + ngz, ngz)
        return (t, row, col)

    first, last = p == 0, p == n - 1
    has_up, has_down = j + 1 < ngz, j >= 1

    barrier = pltpu.get_barrier_semaphore()

    def greet(ok, target):
        @pl.when(ok)
        def _():
            pl.semaphore_signal(barrier, inc=1, device_id=target, device_id_type=MESH)

    for k in range(n):
        t = lax.rem(p + k, n)
        for d in (-1, 0, 1):
            if k or d:
                greet(row_ok(d), dev(t, d, 0))
            greet(row_ok(d) & first & has_down, dev(t, d, -1))
            greet(row_ok(d) & last & has_up, dev(t, d, 1))

    lane = lax.broadcasted_iota(jnp.int32, (rows, LANES), 1)
    sub = lax.broadcasted_iota(jnp.int32, (rows, LANES), 0)

    def roll(x, by):
        if isinstance(by, int):
            by = by % LANES
            return x if by == 0 else pltpu.roll(x, by, 1)
        return pltpu.roll(x, lax.rem(by + 4 * LANES, LANES), 1)

    for load in loads[:3]:
        load.wait()
    for c in range(3):
        cx[c] = drift[c] * (-1.0 / 12.0)
    cx[3] = visc[...]
    plane = jnp.zeros((rows, LANES), jnp.float32)
    for r in range(rows):
        plane = jnp.where(sub == r, offs[r].astype(jnp.float32), plane)
    cx[4] = plane
    low, high = jnp.zeros((rows, LANES), jnp.float32), jnp.zeros((rows, LANES), jnp.float32)
    for c in range(5):
        here = lane // RIM == c
        low = jnp.where(here, roll(cx[c], c * RIM - (LANES - RIM)), low)
        high = jnp.where(here, roll(cx[c], c * RIM), high)
    ch[0] = low
    ch[1] = high

    loads[3].wait()
    for t in range(n):
        for m in range(tiles):
            acc = None
            for s in range(n):
                part = roll(dens[m * n + s], s * width - t * width)
                acc = part if acc is None else jnp.where(lane >= s * width, part, acc)
            tx[t, 1 + m] = acc
        low = high = None
        for q in range(pl_local):
            part_l = roll(dens[q], q * RIM - t * width + RIM)
            part_h = roll(dens[q], q * RIM - t * width - width)
            low = part_l if low is None else jnp.where(lane >= q * RIM, part_l, low)
            high = part_h if high is None else jnp.where(lane >= q * RIM, part_h, high)
        near, far = (high, low) if t == 0 else (low, high)
        tx[t, 0] = near
        tx[t, planes - 1] = far

    expected = jnp.int32(0)
    for d in (-1, 0, 1):
        here = row_ok(d).astype(jnp.int32)
        expected += here * (n - (d == 0))
        expected += here * (j + 1 < ngz).astype(jnp.int32)
        expected += here * (j >= 1).astype(jnp.int32)
    pl.semaphore_wait(barrier, expected)

    def main_copy(k, d):
        t = lax.rem(p + k, n)
        return pltpu.make_async_remote_copy(
            src_ref=tx.at[t, pl.ds(0, count)],
            dst_ref=rx.at[p, 1 - d, pl.ds(0, count)],
            send_sem=s_main.at[k, d + 1], recv_sem=r_main.at[p, 1 - d],
            device_id=dev(t, d, 0), device_id_type=MESH,
        )

    def rim_copy(side, d):
        t, g, at = (0, 1, planes - 1) if side == 0 else (n - 1, -1, planes - 1)
        return pltpu.make_async_remote_copy(
            src_ref=tx.at[t, at], dst_ref=rh.at[p, 1 - d],
            send_sem=s_rim.at[side, d + 1], recv_sem=r_rim.at[p, 1 - d],
            device_id=dev(t, d, g), device_id_type=MESH,
        )

    def coef_copy(d):
        return pltpu.make_async_remote_copy(
            src_ref=cx, dst_ref=rc.at[1 - d],
            send_sem=s_coef.at[d + 1], recv_sem=r_coef.at[1 - d],
            device_id=dev(p, d, 0), device_id_type=MESH,
        )

    def crim_copy(side, d):
        g = 1 if side == 0 else -1
        return pltpu.make_async_remote_copy(
            src_ref=ch.at[side], dst_ref=rch.at[1 - d],
            send_sem=s_crim.at[d + 1], recv_sem=r_crim.at[1 - d],
            device_id=dev(p, d, g), device_id_type=MESH,
        )

    sends = []
    for d in (-1, 1):
        sends.append((row_ok(d), functools.partial(coef_copy, d)))
    for d in (-1, 1, 0):
        sends.append((row_ok(d) & has_up, functools.partial(rim_copy, 0, d)))
        sends.append((row_ok(d) & has_down, functools.partial(rim_copy, 1, d)))
        sends.append((row_ok(d) & has_up & first, functools.partial(crim_copy, 0, d)))
        sends.append((row_ok(d) & has_down & last, functools.partial(crim_copy, 1, d)))
    for k in list(range(1, n)) + [0]:
        for d in (-1, 1, 0):
            if k or d:
                sends.append((row_ok(d), functools.partial(main_copy, k, d)))
    for ok, make in sends:
        @pl.when(ok)
        def _():
            make().start()

    def await_copy(ok, dst, sem):
        @pl.when(ok)
        def _():
            pltpu.make_async_copy(dst, dst, sem).wait()

    out_ok = (first & has_down) | (last & has_up)
    row_at = i * rows + sub
    hgt_at = j * LANES + p * width + lane - RIM
    hgt_in = (hgt_at >= 0) & (hgt_at < ngz * LANES)

    def inside(slot):
        at = row_at + (slot - 1) * rows
        return hgt_in & (at >= 0) & (at < nrow * rows)

    low_side, high_side = lane < RIM, lane >= RIM + width
    swap = (low_side & first) | (high_side & last)

    for slot in (1, 0, 2):
        ok = row_ok(slot - 1)
        if slot != 1:
            await_copy(ok, rc.at[slot], r_coef.at[slot])
        await_copy(ok & out_ok, rch.at[slot], r_crim.at[slot])
        base = jnp.where(first, 0, RIM + width)
        for c in range(5):
            body = cx[c] if slot == 1 else rc[slot, c]
            value = jnp.where(
                swap, roll(rch[slot], base - c * RIM), roll(body, RIM - p * width)
            )
            coef[c, pl.ds(slot * rows, rows)] = jnp.where(inside(slot), value, 0.0)

    for slot in (1, 0, 2):
        ok = row_ok(slot - 1)
        for k in range(n):
            ps = lax.rem(p + k, n)
            mine = k == 0 and slot == 1
            if not mine:
                view = rx.at[ps, slot, pl.ds(0, count)]
                await_copy(ok, view, r_main.at[ps, slot])
            await_copy(ok & out_ok, rh.at[ps, slot], r_rim.at[ps, slot])

            def got(m):
                return tx[p, m] if mine else rx[ps, slot, m]

            rim = rh[ps, slot]
            low = jnp.where(first, rim, got(0))
            high = jnp.where(first, got(0), rim)
            if n > 2:
                high = jnp.where(first | last, high, got(planes - 1))
            for q in range(pl_local):
                m, s = q // n, q % n
                value = jnp.where(
                    low_side, roll(low, -q * RIM),
                    jnp.where(
                        high_side, roll(high, RIM + width - q * RIM),
                        roll(got(1 + m), RIM - s * width),
                    ),
                )
                ext[2 + ps * pl_local + q, pl.ds(slot * rows, rows)] = jnp.where(
                    inside(slot), value, 0.0
                )

    def section(src, dst, r0, size, combine):
        e0, e1, e2, nu = (coef[c, pl.ds(r0, size)] for c in range(4))

        def body(a, carry):
            def at(k, d=0):
                return src[a + 2 + k, pl.ds(r0 + d, size)]

            c = at(0)
            a1, b1, a2, b2 = at(1), at(-1), at(2), at(-2)
            u1, d1, u2, d2 = at(0, 1), at(0, -1), at(0, 2), at(0, -2)
            g1, h1 = pltpu.roll(c, LANES - 1, 1), pltpu.roll(c, 1, 1)
            g2, h2 = pltpu.roll(c, LANES - 2, 1), pltpu.roll(c, 2, 1)
            change = e0 * (8.0 * (a1 - b1) - (a2 - b2))
            change += e1 * (8.0 * (u1 - d1) - (u2 - d2))
            change += e2 * (8.0 * (g1 - h1) - (g2 - h2))
            change += nu * (((a1 + b1) + (u1 + d1)) + (g1 + h1) - 6.0 * c)
            dst[a + 2, pl.ds(r0, size)] = combine(a, c + change)
            return carry

        lax.fori_loop(0, nphi, body, 0, unroll=16 if nphi % 16 == 0 else 1)

    def wrap(ref, r0, size):
        at = pl.ds(r0, size)
        ref[pl.ds(0, 2), at] = ref[pl.ds(nphi, 2), at]
        ref[pl.ds(nphi + 2, 2), at] = ref[pl.ds(2, 2), at]

    def rotated(r0):
        value = one[pl.ds(2, nphi), pl.ds(r0, 8)]
        turns = coef[4, pl.ds(r0, 8)].astype(jnp.int32)
        span = 1
        while span < nphi:
            moved = jnp.concatenate([value[nphi - span :], value[: nphi - span]], axis=0)
            value = jnp.where(((turns & span) != 0)[None], moved, value)
            span *= 2
        return value

    for step, (ra, rb, rd) in enumerate((((4, 40), (8, 32), (8, 32)), ((12, 24), (12, 24), (16, 16)))):
        wrap(ext, *ra)
        section(ext, one, *ra, lambda a, v: v)
        wrap(one, *ra)
        section(
            one, two, *rb, lambda a, v: 0.75 * ext[a + 2, pl.ds(rb[0], rb[1])] + 0.25 * v
        )
        wrap(two, *rb)
        section(
            two, one, *rd,
            lambda a, v: ext[a + 2, pl.ds(rd[0], rd[1])] * (1.0 / 3.0) + (2.0 / 3.0) * v,
        )
        for r0 in range(rd[0], rd[0] + rd[1], 8):
            ext[pl.ds(2, nphi), pl.ds(r0, 8)] = rotated(r0)

    def out_copy(k):
        t = lax.rem(p + k, n)
        return pltpu.make_async_remote_copy(
            src_ref=txo.at[k], dst_ref=rxo.at[p],
            send_sem=s_out.at[k], recv_sem=r_out.at[p],
            device_id=dev(t, 0, 0), device_id_type=MESH,
        )

    for k in range(1, n):
        t = lax.rem(p + k, n)
        for m in range(tiles):
            acc = None
            for s in range(n):
                part = roll(
                    ext[2 + t * pl_local + m * n + s, pl.ds(rows, rows)], s * width - RIM
                )
                acc = part if acc is None else jnp.where(lane >= s * width, part, acc)
            txo[k, m] = acc
        out_copy(k).start()

    for q in range(pl_local):
        out[q] = roll(ext[2 + p * pl_local + q, pl.ds(rows, rows)], p * width - RIM)
    for k in range(1, n):
        ps = lax.rem(p + k, n)
        await_copy(True, rxo.at[ps], r_out.at[ps])
        here = (lane >= ps * width) & (lane < (ps + 1) * width)
        for q in range(pl_local):
            m, s = q // n, q % n
            out[q] = jnp.where(here, roll(rxo[ps, m], ps * width - s * width), out[q])
    for ok, make in sends:
        @pl.when(ok)
        def _():
            make().wait_send()
    for k in range(1, n):
        out_copy(k).wait_send()


def local(sizes, density, drift_speed, viscosity, offsets):
    n = sizes[0]
    pl_local, rows, lanes = density.shape
    tiles = pl_local // n
    planes = tiles + 2
    nphi = n * pl_local
    f32 = jnp.float32
    block = (rows, lanes)
    deep = (3 * rows, lanes)
    vmem = pl.BlockSpec(memory_space=pltpu.VMEM)
    dma = pltpu.SemaphoreType.DMA
    return pl.pallas_call(
        functools.partial(kernel, sizes),
        out_shape=jax.ShapeDtypeStruct(density.shape, f32),
        in_specs=[pl.BlockSpec(memory_space=pltpu.HBM)] * 4,
        out_specs=vmem,
        scratch_shapes=[
            pltpu.VMEM(density.shape, f32),
            pltpu.VMEM(drift_speed.shape, f32),
            pltpu.VMEM(viscosity.shape, f32),
            pltpu.SMEM(offsets.shape, jnp.int32),
            dma((4,)),
            pltpu.VMEM((n, planes) + block, f32),
            pltpu.VMEM((n, 3, planes) + block, f32),
            pltpu.VMEM((n, 3) + block, f32),
            pltpu.VMEM((5,) + block, f32),
            pltpu.VMEM((3, 5) + block, f32),
            pltpu.VMEM((2,) + block, f32),
            pltpu.VMEM((3,) + block, f32),
            pltpu.VMEM((nphi + 4,) + deep, f32),
            pltpu.VMEM((nphi + 4,) + deep, f32),
            pltpu.VMEM((nphi + 4,) + deep, f32),
            pltpu.VMEM((5,) + deep, f32),
            pltpu.VMEM((n, tiles) + block, f32),
            pltpu.VMEM((n, tiles) + block, f32),
            dma((n, 3)), dma((n, 3)), dma((2, 3)), dma((n, 3)), dma((3,)), dma((3,)),
            dma((3,)), dma((3,)), dma((n,)), dma((n,)),
        ],
        compiler_params=pltpu.CompilerParams(
            collective_id=0, has_side_effects=True, vmem_limit_bytes=60 * 1024 * 1024
        ),
    )(density, drift_speed, viscosity, offsets)


def solution(mesh):
    sizes = (mesh.shape["phi"], mesh.shape["row"], mesh.shape["gz"])
    in_specs = (P("phi", "row", "gz"), P(None, "row", "gz"), P("row", "gz"), P("row"))
    return jax.shard_map(
        functools.partial(local, sizes), mesh=mesh, in_specs=in_specs,
        out_specs=P("phi", "row", "gz"), check_vma=False,
    )
```
